32 devices in a mesh: grp: 2 (over x), dp: 16 (over z, y, core).
Axes of the slice: x: 2, y: 2, z: 4, core: 2. Of those that a mesh axis runs over, the one named last changes fastest.
Arguments:
- tokens_in: bfloat16 [8192, 1024], P(('grp', 'dp')), may hold values from -6 to 6
- grad_out: bfloat16 [8192, 1024], P(('grp', 'dp')), may hold values from -6 to 6
- seq_lengths: int32 [16, 16], P('dp'), may hold values from 1 to 125, as said below
- seq_deal: int32 [16, 16], P('dp'), may hold values from 0 to 15, as said below
- norm_attn: bfloat16 [1024], P(('grp', 'dp')), may hold values from 0.099609375 to 1.8984375
- query_key_value_weight: bfloat16 [1024, 4096], P(('grp', 'dp')), may hold values from -0.1875 to 0.1875
- query_norm_gain: bfloat16 [128], P(('grp', 'dp')), may hold values from 0.099609375 to 1.8984375
- k_gain: bfloat16 [128], P(('grp', 'dp')), may hold values from 0.099609375 to 1.8984375
- output_weight: bfloat16 [2048, 1024], P(('grp', 'dp')), may hold values from -0.375 to 0.375
- norm_mlp: bfloat16 [1024], P(('grp', 'dp')), may hold values from 0.099609375 to 1.8984375
- w_gate_up: bfloat16 [1024, 6144], P(('grp', 'dp')), may hold values from -0.1875 to 0.1875
- w_down: bfloat16 [3072, 1024], P(('grp', 'dp')), may hold values from -0.109375 to 0.109375
Outputs:
- y_out: bfloat16 [8192, 1024], P(('grp', 'dp'))
- grad_in: float32 [8192, 1024], P(('grp', 'dp'))
- grad_norm_attn: float32 [1024], P(('grp', 'dp'))
- grad_qkv: float32 [1024, 4096], P(('grp', 'dp'))
- grad_q_gain: float32 [128], P(('grp', 'dp'))
- grad_k_gain: float32 [128], P(('grp', 'dp'))
- grad_out_proj: float32 [2048, 1024], P(('grp', 'dp'))
- grad_norm_mlp: float32 [1024], P(('grp', 'dp'))
- grad_gate_up: float32 [1024, 6144], P(('grp', 'dp'))
- grad_down: float32 [3072, 1024], P(('grp', 'dp'))
The draws below stay inside these ranges and needn't reach their ends.
Inputs may be any that keep to these rules, and one draw needn't show every extreme that they name: `seq_lengths`: each row sums to 512. `seq_deal`: each row is a permutation; for each grp index c and micro-batch m, the sequences in slots (c * 2 + m) * 4 + j, j below 4, have lengths that sum to 128.
All inputs are finite; a program needn't handle non-finite values.
Results may differ from the reference program's by a relative error of at most 0.015.
Values may be sent and summed in bfloat16 or wider, within the bound.
No kernel may reach another device: no remote copies, remote signals or barrier semaphores. Data moves between devices by JAX's collectives and lax.ppermute only.
A program may use at most 192 MiB of HBM per device.

```python
import jax
import jax.numpy as jnp
from jax import lax

MODEL_WIDTH = 1024
QUERY_HEADS = 16
KEY_VALUE_HEADS = 8
HEAD_SIZE = 128
FF = 3072
MB_TOK = 128
SEQ_GROUP = 4
TOK_DEV = 256
SEQ_PAIR = 16
TOKENS = 8192
N_GRP = 2
N_DP = 16


def deal_plan(key):
    base = jax.random.fold_in(key, 11)
    groups = SEQ_PAIR // SEQ_GROUP
    token_count = N_DP * groups
    cut_scores = jax.random.randint(jax.random.fold_in(base, 1), (token_count, MB_TOK - 1), 0, 1 << 20) * MB_TOK + jnp.arange(MB_TOK - 1, dtype=jnp.int32)[None, :]
    chosen = lax.top_k(cut_scores, SEQ_GROUP - 1)[1].astype(jnp.int32) + 1
    forced = jnp.arange(1, SEQ_GROUP, dtype=jnp.int32)
    chosen = jnp.where((jnp.arange(token_count) == 0)[:, None], forced[None, :], chosen)
    cuts = jnp.sort(chosen, axis=1)
    edges = jnp.concatenate([jnp.zeros((token_count, 1), jnp.int32), cuts, jnp.full((token_count, 1), MB_TOK, jnp.int32)], axis=1)
    dealt_lengths = (edges[:, 1:] - edges[:, :-1]).reshape(N_DP, SEQ_PAIR)
    order_scores = jax.random.randint(jax.random.fold_in(base, 2), (N_DP, SEQ_PAIR), 0, 1 << 20) * SEQ_PAIR + jnp.arange(SEQ_PAIR, dtype=jnp.int32)[None, :]
    deal_order = jnp.argsort(order_scores, axis=1, stable=True).astype(jnp.int32)
    inverse = jnp.argsort(deal_order, axis=1, stable=True)
    source_lengths = jnp.take_along_axis(dealt_lengths, inverse, axis=1)
    return (source_lengths.astype(jnp.int32), deal_order)


def draw_seq_lengths(key, part):
    return deal_plan(key)[0]


def draw_seq_deal(key, part):
    return deal_plan(key)[1]


def steps_of(rng, extent, split, least, largest):
    factor_of, own = 1.0, jax.random.fold_in(rng, 6)
    for dim, blocks in split:
        draws = jnp.exp(jax.random.uniform(jax.random.fold_in(own, dim), (blocks,), jnp.float32, least / len(split), largest / len(split)))
        factor_of = factor_of * jnp.repeat(draws, extent[dim] // blocks).reshape([-1 if axis == dim else 1 for axis in range(len(extent))])
    return factor_of


def gaussian(stream_key, shape, deviation, bound, cuts=(), kind=jnp.bfloat16):
    values = jax.random.normal(stream_key, shape, jnp.float32) * deviation
    if len(cuts) > 0:
        values = steps_of(stream_key, shape, cuts, -0.22, 0.18) * values
    return jnp.clip(values, min=-bound, max=bound).astype(kind)


def setup_inputs(seed: int = 0) -> dict:
    keys = jax.random.split(jax.random.key(seed), 13)
    return {
        "tokens_in": gaussian(keys[0], (TOKENS, MODEL_WIDTH), 1.0, 6.0, ((0, 32),)),
        "grad_out": gaussian(keys[1], (TOKENS, MODEL_WIDTH), 1.0, 6.0, ((0, 32),)),
        "seq_lengths": draw_seq_lengths(jax.random.fold_in(keys[12], 71), 0),
        "seq_deal": draw_seq_deal(jax.random.fold_in(keys[12], 71), 0),
        "norm_attn": jnp.clip(1.0 + 0.18 * jax.random.normal(keys[4], (MODEL_WIDTH,), jnp.float32), 0.099609375, 1.8984375).astype(jnp.bfloat16),
        "query_key_value_weight": gaussian(keys[5], (MODEL_WIDTH, (QUERY_HEADS + 2 * KEY_VALUE_HEADS) * HEAD_SIZE), MODEL_WIDTH ** -0.5, 0.1875, ((0, 32),)),
        "query_norm_gain": jnp.clip(1.0 + 0.18 * jax.random.normal(keys[6], (HEAD_SIZE,), jnp.float32), 0.099609375, 1.8984375).astype(jnp.bfloat16),
        "k_gain": jnp.clip(1.0 + 0.18 * jax.random.normal(keys[7], (HEAD_SIZE,), jnp.float32), 0.099609375, 1.8984375).astype(jnp.bfloat16),
        "output_weight": gaussian(keys[8], (QUERY_HEADS * HEAD_SIZE, MODEL_WIDTH), (QUERY_HEADS * HEAD_SIZE // 8) ** -0.5, 0.375, ((0, 32),)),
        "norm_mlp": jnp.clip(1.0 + 0.18 * jax.random.normal(keys[9], (MODEL_WIDTH,), jnp.float32), 0.099609375, 1.8984375).astype(jnp.bfloat16),
        "w_gate_up": gaussian(keys[10], (MODEL_WIDTH, 2 * FF), MODEL_WIDTH ** -0.5, 0.1875, ((0, 32),)),
        "w_down": gaussian(keys[11], (FF, MODEL_WIDTH), FF ** -0.5, 0.109375, ((0, 32),)),
    }


EPSILON = 1e-06
ROPE_BASE = 1000000.0
MASKED = -1e+30
HIGHEST = lax.Precision.HIGHEST

@jax.custom_vjp
def reduced_precision(v):
    return lax.optimization_barrier(v.astype(jnp.bfloat16)).astype(jnp.float32)

@jax.custom_vjp
def low_back(v):
    return v

def low_keep(v):
    return (reduced_precision(v), None)

def low_pass(kept, grad):
    return (grad,)

def back_keep(v):
    return (v, None)

def back_low(kept, grad):
    return (reduced_precision(grad),)
reduced_precision.defvjp(low_keep, low_pass)
low_back.defvjp(back_keep, back_low)

def deal_slots(lengths, deal_order):
    token_count = lengths.shape[0]
    seq_ids = jnp.arange(token_count, dtype=jnp.int32)
    starts = (jnp.cumsum(lengths) - lengths).astype(jnp.int32)
    pick = (deal_order[:, None] == seq_ids[None, :]).astype(jnp.int32)
    slot_length = lax.optimization_barrier(jnp.sum(pick * lengths[None, :], axis=1)).astype(jnp.int32)
    slot_source = lax.optimization_barrier(jnp.sum(pick * starts[None, :], axis=1)).astype(jnp.int32)
    groups = token_count // SEQ_GROUP
    grouped = slot_length.reshape(groups, SEQ_GROUP)
    offsets = (jnp.cumsum(grouped, axis=1) - grouped).astype(jnp.int32)
    slot_dealt = (offsets + jnp.arange(groups, dtype=jnp.int32)[:, None] * MB_TOK).reshape(token_count).astype(jnp.int32)
    return (seq_ids, slot_length, slot_source, slot_dealt)

def deal_rows(lengths, deal_order):
    seq_ids, slot_length, slot_source, slot_dealt = deal_slots(lengths, deal_order)
    total_rows = lengths.shape[0] // SEQ_GROUP * MB_TOK
    rows = jnp.arange(total_rows, dtype=jnp.int32)
    inside = ((rows[:, None] >= slot_dealt[None, :]) & (rows[:, None] < (slot_dealt + slot_length)[None, :])).astype(jnp.int32)
    source = (rows + lax.optimization_barrier(jnp.sum(inside * (slot_source - slot_dealt)[None, :], axis=1))).astype(jnp.int32)
    segment = lax.optimization_barrier(jnp.sum(inside * seq_ids[None, :], axis=1)).astype(jnp.int32)
    position = (rows - lax.optimization_barrier(jnp.sum(inside * slot_dealt[None, :], axis=1))).astype(jnp.int32)
    return (source, segment, position)

def root_mean_scale(values):
    return lax.rsqrt(lax.optimization_barrier(jnp.mean(values * values, axis=-1, keepdims=True)) + EPSILON)

def rope_tables(position):
    half_width = HEAD_SIZE // 2
    frequency = ROPE_BASE ** (-2.0 * jnp.arange(half_width, dtype=jnp.float32) / HEAD_SIZE)
    angles = position.astype(jnp.float32)[:, None] * frequency[None, :]
    cosine_table = jnp.concatenate([jnp.cos(angles), jnp.cos(angles)], axis=-1)[:, None, :]
    sine_table = jnp.concatenate([jnp.sin(angles), jnp.sin(angles)], axis=-1)[:, None, :]
    return (cosine_table, sine_table)

def apply_rotation(inputs, cosine_table, sine_table):
    half_width = inputs.shape[-1] // 2
    turned = jnp.concatenate([-inputs[..., half_width:], inputs[..., :half_width]], axis=-1)
    return inputs * cosine_table + turned * sine_table

def pair_layer(x_pair, segment, position, norm_one, query_key_value_weight, query_norm_gain, k_gain, output_weight, norm_two, w_gate_up, w_down):
    token_count = x_pair.shape[0]
    query_width = QUERY_HEADS * HEAD_SIZE
    key_value_width = KEY_VALUE_HEADS * HEAD_SIZE
    query_group_size = QUERY_HEADS // KEY_VALUE_HEADS
    scale_one = root_mean_scale(x_pair)
    normed_one = reduced_precision(x_pair * scale_one * norm_one)
    projected_output = low_back(jnp.dot(normed_one, query_key_value_weight, precision=HIGHEST))
    query_rows = projected_output[:, :query_width].reshape(token_count, QUERY_HEADS, HEAD_SIZE)
    unnormed_keys = projected_output[:, query_width:query_width + key_value_width].reshape(token_count, KEY_VALUE_HEADS, HEAD_SIZE)
    value_reduced = reduced_precision(projected_output[:, query_width + key_value_width:]).reshape(token_count, KEY_VALUE_HEADS, HEAD_SIZE)
    cosine_table, sine_table = rope_tables(position)
    query_reduced = reduced_precision(apply_rotation(query_rows * root_mean_scale(query_rows) * query_norm_gain, cosine_table, sine_table)).reshape(token_count, KEY_VALUE_HEADS, query_group_size, HEAD_SIZE)
    key_low = reduced_precision(apply_rotation(unnormed_keys * root_mean_scale(unnormed_keys) * k_gain, cosine_table, sine_table))
    allowed = (segment[:, None] == segment[None, :]) & (position[None, :] <= position[:, None])
    scores = low_back(jnp.einsum('tkgd,skd->kgts', query_reduced, key_low, precision=HIGHEST) * HEAD_SIZE ** (-0.5))
    scores = jnp.where(allowed[None, None], scores, MASKED)
    top_score = lax.optimization_barrier(jnp.max(scores, axis=-1, keepdims=True))
    expo = jnp.exp(scores - top_score)
    probs = reduced_precision(expo / lax.optimization_barrier(jnp.sum(expo, axis=-1, keepdims=True)))
    mixed = jnp.einsum('kgts,skd->tkgd', probs, value_reduced, precision=HIGHEST).reshape(token_count, query_width)
    attended = low_back(reduced_precision(mixed))
    residual = x_pair + low_back(jnp.dot(attended, output_weight, precision=HIGHEST))
    normed_two = reduced_precision(residual * root_mean_scale(residual) * norm_two)
    gate_up = low_back(jnp.dot(normed_two, w_gate_up, precision=HIGHEST))
    activated = reduced_precision(jax.nn.silu(gate_up[:, :FF]) * gate_up[:, FF:])
    return residual + low_back(jnp.dot(activated, w_down, precision=HIGHEST))

def reference(tokens_in, grad_out, seq_lengths, seq_deal, norm_attn, query_key_value_weight, query_norm_gain, k_gain, output_weight, norm_mlp, w_gate_up, w_down):
    pairs = seq_lengths.shape[0]
    pair_rows = N_GRP * TOK_DEV
    source, segment, position = jax.vmap(deal_rows)(seq_lengths, seq_deal)

    def to_pairs(array):
        return array.reshape(N_GRP, pairs, TOK_DEV, array.shape[-1]).transpose(1, 0, 2, 3).reshape(pairs, pair_rows, array.shape[-1])

    def from_pairs(array):
        return array.reshape(pairs, N_GRP, TOK_DEV, array.shape[-1]).transpose(1, 0, 2, 3).reshape(N_GRP * pairs * TOK_DEV, array.shape[-1])
    layer = jax.checkpoint(pair_layer)

    def whole(x_float, norm_one, qkv_float, gain_q, gain_k, out_float, norm_two, gate_float, down_float):
        paired = to_pairs(x_float)
        dealt = jnp.take_along_axis(paired, source[:, :, None], axis=1)

        def one_pair(pieces):
            return layer(pieces[0], pieces[1], pieces[2], norm_one, qkv_float, gain_q, gain_k, out_float, norm_two, gate_float, down_float)
        outputs = lax.map(one_pair, (dealt, segment, position))
        return from_pairs(outputs)
    floats = (tokens_in.astype(jnp.float32), norm_attn.astype(jnp.float32), query_key_value_weight.astype(jnp.float32), query_norm_gain.astype(jnp.float32), k_gain.astype(jnp.float32), output_weight.astype(jnp.float32), norm_mlp.astype(jnp.float32), w_gate_up.astype(jnp.float32), w_down.astype(jnp.float32))
    output, pullback = jax.vjp(whole, *floats)
    grads = pullback(grad_out.astype(jnp.float32))
    return (output.astype(jnp.bfloat16), grads[0], grads[1], grads[2], grads[3], grads[4], grads[5], grads[6], grads[7], grads[8])
```

```python
import jax
import jax.numpy as jnp
from jax import lax
from jax.experimental import pallas as pl
from jax.experimental.pallas import tpu as pltpu
from jax.sharding import PartitionSpec as P

QUERY_HEADS = 16
KEY_VALUE_HEADS = 8
HEAD_SIZE = 128
FF = 3072
MB_TOK = 128
SEQ_GROUP = 4

EPSILON = 1e-06
ROPE_BASE = 1000000.0
MASKED = -1e30
SCALE = HEAD_SIZE**-0.5
QUERIES_PER_KEY = QUERY_HEADS // KEY_VALUE_HEADS

BF16 = jnp.bfloat16
F32 = jnp.float32


def deal_slots(lengths, deal_order):
    token_count = lengths.shape[0]
    seq_ids = jnp.arange(token_count, dtype=jnp.int32)
    starts = jnp.cumsum(lengths) - lengths
    pick = (deal_order[:, None] == seq_ids[None, :]).astype(jnp.int32)
    slot_length = jnp.sum(pick * lengths[None, :], axis=1)
    slot_source = jnp.sum(pick * starts[None, :], axis=1)
    groups = token_count // SEQ_GROUP
    grouped = slot_length.reshape(groups, SEQ_GROUP)
    offsets = jnp.cumsum(grouped, axis=1) - grouped
    slot_dealt = (offsets + jnp.arange(groups, dtype=jnp.int32)[:, None] * MB_TOK).reshape(
        token_count
    )
    return (seq_ids, starts, pick, slot_length, slot_source, slot_dealt)


def deal_rows(lengths, deal_order, rows):
    _, _, _, slot_length, slot_source, slot_dealt = deal_slots(lengths, deal_order)
    inside = (
        (rows[:, None] >= slot_dealt[None, :])
        & (rows[:, None] < (slot_dealt + slot_length)[None, :])
    ).astype(jnp.int32)
    source = rows + jnp.sum(inside * (slot_source - slot_dealt)[None, :], axis=1)
    position = rows - jnp.sum(inside * slot_dealt[None, :], axis=1)
    return (source, position)


def back_rows(lengths, deal_order, rows):
    _, starts, pick, _, _, slot_dealt = deal_slots(lengths, deal_order)
    seq_dealt = jnp.sum(pick * slot_dealt[:, None], axis=0)
    inside = (
        (rows[:, None] >= starts[None, :]) & (rows[:, None] < (starts + lengths)[None, :])
    ).astype(jnp.int32)
    return rows + jnp.sum(inside * (seq_dealt - starts)[None, :], axis=1)


def take_rows(own, peer, rows, first_row):
    half = own.shape[0]
    near = jnp.remainder(rows - first_row, 2 * half)
    lane = lax.broadcasted_iota(jnp.int32, (rows.shape[0], half), 1)
    pick_own = (near[:, None] == lane).astype(own.dtype)
    pick_peer = (near[:, None] == lane + half).astype(own.dtype)
    return jnp.dot(pick_own, own, preferred_element_type=F32) + jnp.dot(
        pick_peer, peer, preferred_element_type=F32
    )


def swap(values, axis, mask):
    size = lax.axis_size(axis)
    return lax.ppermute(values, axis, [(i, i ^ mask) for i in range(size)])


def swap_core(values):
    return swap(values, "dp", 1)


def swap_y(values):
    return swap(values, "dp", 2)


def swap_z(values, step):
    return swap(values, "dp", 4 * step)


def swap_x(values):
    return swap(values, "grp", 1)


class Place:
    def __init__(self):
        index = lax.axis_index("dp")
        self.x = lax.axis_index("grp")
        self.core = index % 2
        self.y = (index // 2) % 2
        self.z = index // 4
        self.depth = lax.axis_size("dp") // 4
        self.chips = lax.axis_size("dp")


def ordered(bit, own, peer, axis):
    return jnp.where(
        bit == 0,
        jnp.concatenate([own, peer], axis=axis),
        jnp.concatenate([peer, own], axis=axis),
    )


def pick(values, index, axis):
    return lax.dynamic_index_in_dim(values, index, axis, keepdims=False)


def paired(bit, own, peer, axis):
    return ordered(bit, jnp.expand_dims(own, axis), jnp.expand_dims(peer, axis), axis)


def by_z(place, pieces, axis):
    step = 1
    groups = [jnp.expand_dims(piece, axis) for piece in pieces]
    while step < place.depth:
        bit = (place.z // step) % 2
        groups = [
            ordered(bit, groups[2 * i], groups[2 * i + 1], axis) for i in range(len(groups) // 2)
        ]
        step *= 2
    return groups[0]


def spread_z(place, piece, axis):
    pieces = [piece] + [swap_z(piece, step) for step in range(1, place.depth)]
    return by_z(place, pieces, axis)


def gather_late_x(place, stack):
    stack = paired(place.y, stack, swap_y(stack), 1)
    stack = paired(place.x, stack, swap_x(stack), 0)
    return stack.reshape(-1, stack.shape[-1])


def gather_late_y(place, stack):
    stack = paired(place.x, stack, swap_x(stack), 0)
    stack = paired(place.y, stack, swap_y(stack), 2)
    return stack.reshape(-1, stack.shape[-1])


def gather_halves(place, piece):
    half = piece.shape[1] // 2
    stack = spread_z(place, piece, 0)
    return (
        gather_late_x(place, stack[..., :half]),
        gather_late_y(place, stack[..., half:]),
    )


def gather_late_z(place, piece):
    half = piece.shape[1] // 2
    first, second = piece[:, :half], piece[:, half:]
    first = paired(place.x, first, swap_x(first), 0)
    first = paired(place.y, first, swap_y(first), 1)
    second = paired(place.y, second, swap_y(second), 0)
    second = paired(place.x, second, swap_x(second), 0)
    both = jnp.concatenate([first, second], axis=-1)
    stack = spread_z(place, both, 1)
    return stack.reshape(-1, stack.shape[-1])


def add(first, second):
    return (first.astype(F32) + second.astype(F32)).astype(BF16)


def scatter_plane(place, grads, first):
    depth = place.depth
    rows = grads.shape[0] // (4 * depth)
    grads = grads.reshape(2, depth, 2, rows, grads.shape[1])
    if first == "x":
        part = add(pick(grads, place.x, 0), swap_x(pick(grads, 1 - place.x, 0)))
        return add(pick(part, place.y, 1), swap_y(pick(part, 1 - place.y, 1)))
    part = add(pick(grads, place.y, 2), swap_y(pick(grads, 1 - place.y, 2)))
    return add(pick(part, place.x, 0), swap_x(pick(part, 1 - place.x, 0)))


def scatter_z(place, part):
    total = pick(part, place.z, 0).astype(F32)
    for step in range(1, place.depth):
        total = total + swap_z(pick(part, place.z ^ step, 0), step).astype(F32)
    return total


def scatter_halves(place, grads_a, grads_b):
    part = jnp.concatenate(
        [scatter_plane(place, grads_a, "x"), scatter_plane(place, grads_b, "y")], axis=-1
    )
    return scatter_z(place, part)


def gather_small(place, row):
    stack = ordered(place.core, row, swap_core(row), 0)
    stack = spread_z(place, stack, 0)
    stack = paired(place.y, stack, swap_y(stack), 1)
    stack = paired(place.x, stack, swap_x(stack), 0)
    return stack.reshape(-1, row.shape[1])


def scatter_small(place, rows):
    grads = rows.reshape(2, place.depth, 2, 2, rows.shape[1])
    grads = pick(grads, place.core, 3) + swap_core(pick(grads, 1 - place.core, 3))
    grads = pick(grads, place.x, 0) + swap_x(pick(grads, 1 - place.x, 0))
    grads = pick(grads, place.y, 1) + swap_y(pick(grads, 1 - place.y, 1))
    total = pick(grads, place.z, 0)
    for step in range(1, place.depth):
        total = total + swap_z(pick(grads, place.z ^ step, 0), step)
    return total


def rope(values, cosine, sine):
    return values * cosine + pltpu.roll(values, HEAD_SIZE // 2, 1) * sine


def rope_back(grads, cosine, sine):
    return grads * cosine + pltpu.roll(grads * sine, HEAD_SIZE // 2, 1)


def row_scale(values):
    return lax.rsqrt(jnp.mean(values * values, axis=-1, keepdims=True) + EPSILON)


def head(ref, index):
    return ref[:, index * HEAD_SIZE : (index + 1) * HEAD_SIZE]


def dot_t(left, right):
    return lax.dot_general(left, right, (((1,), (1,)), ((), ())), preferred_element_type=F32)


def t_dot(left, right):
    return lax.dot_general(left, right, (((0,), (0,)), ((), ())), preferred_element_type=F32)


def allowed_keys(position):
    row = lax.broadcasted_iota(jnp.int32, (MB_TOK, MB_TOK), 0)
    key = lax.broadcasted_iota(jnp.int32, (MB_TOK, MB_TOK), 1)
    allowed = (key <= row) & (key >= row - position)
    return jnp.concatenate([allowed] * QUERIES_PER_KEY, axis=0)


def attend_kernel(q_ref, kv_ref, cos_ref, sin_ref, pos_ref, qg_ref, kg_ref, out_ref):
    heads = kv_ref.shape[1] // (2 * HEAD_SIZE)
    cosine, sine = cos_ref[...], sin_ref[...]
    allowed = allowed_keys(pos_ref[...])
    for j in range(heads):
        keys = head(kv_ref, j)
        key_low = rope(keys * row_scale(keys) * kg_ref[...], cosine, sine).astype(BF16)
        value = head(kv_ref, heads + j).astype(BF16)
        queries = []
        for g in range(QUERIES_PER_KEY):
            query = head(q_ref, QUERIES_PER_KEY * j + g)
            queries.append(
                rope(query * row_scale(query) * qg_ref[...], cosine, sine).astype(BF16)
            )
        scores = dot_t(jnp.concatenate(queries, axis=0), key_low) * SCALE
        scores = jnp.where(allowed, scores, MASKED)
        expo = jnp.exp(scores - jnp.max(scores, axis=-1, keepdims=True))
        probs = (expo / jnp.sum(expo, axis=-1, keepdims=True)).astype(BF16)
        mixed = jnp.dot(probs, value, preferred_element_type=F32).astype(BF16)
        for g in range(QUERIES_PER_KEY):
            index = QUERIES_PER_KEY * j + g
            out_ref[:, index * HEAD_SIZE : (index + 1) * HEAD_SIZE] = mixed[
                g * MB_TOK : (g + 1) * MB_TOK
            ]


def attend_back_kernel(
    q_ref, kv_ref, cos_ref, sin_ref, pos_ref, qg_ref, kg_ref, datt_ref,
    dq_ref, dkv_ref, sum_q_ref, sum_k_ref,
):
    heads = kv_ref.shape[1] // (2 * HEAD_SIZE)
    cosine, sine = cos_ref[...], sin_ref[...]
    allowed = allowed_keys(pos_ref[...])

    @pl.when(pl.program_id(0) == 0)
    def _():
        sum_q_ref[...] = jnp.zeros_like(sum_q_ref)
        sum_k_ref[...] = jnp.zeros_like(sum_k_ref)

    def normed_back(grad_low, raw, scale, gain):
        grad = rope_back(grad_low, cosine, sine)
        term = jnp.sum((grad * raw * scale).reshape(-1, 8, HEAD_SIZE), axis=0)
        weighted = grad * gain
        back = scale * weighted - raw * (scale * scale * scale) * jnp.mean(
            weighted * raw, axis=-1, keepdims=True
        )
        return back, term

    for j in range(heads):
        keys = head(kv_ref, j)
        key_scale = row_scale(keys)
        key_low = rope(keys * key_scale * kg_ref[...], cosine, sine).astype(BF16)
        value = head(kv_ref, heads + j).astype(BF16)
        raws, scales, lows, datts = [], [], [], []
        for g in range(QUERIES_PER_KEY):
            query = head(q_ref, QUERIES_PER_KEY * j + g)
            scale = row_scale(query)
            raws.append(query)
            scales.append(scale)
            lows.append(rope(query * scale * qg_ref[...], cosine, sine).astype(BF16))
            datts.append(head(datt_ref, QUERIES_PER_KEY * j + g))
        low = jnp.concatenate(lows, axis=0)
        datt = jnp.concatenate(datts, axis=0)
        scores = jnp.where(allowed, dot_t(low, key_low) * SCALE, MASKED)
        expo = jnp.exp(scores - jnp.max(scores, axis=-1, keepdims=True))
        probs = expo / jnp.sum(expo, axis=-1, keepdims=True)
        dprobs = dot_t(datt, value)
        dscores = (
            probs * (dprobs - jnp.sum(probs * dprobs, axis=-1, keepdims=True))
        ).astype(BF16)
        dlow = jnp.dot(dscores, key_low, preferred_element_type=F32) * SCALE
        dkey = t_dot(dscores, low) * SCALE
        dvalue = t_dot(probs.astype(BF16), datt)
        for g in range(QUERIES_PER_KEY):
            index = QUERIES_PER_KEY * j + g
            back, term = normed_back(
                dlow[g * MB_TOK : (g + 1) * MB_TOK], raws[g], scales[g], qg_ref[...]
            )
            dq_ref[:, index * HEAD_SIZE : (index + 1) * HEAD_SIZE] = back.astype(BF16)
            sum_q_ref[...] += term
        back, term = normed_back(dkey, keys, key_scale, kg_ref[...])
        dkv_ref[:, j * HEAD_SIZE : (j + 1) * HEAD_SIZE] = back.astype(BF16)
        sum_k_ref[...] += term
        index = heads + j
        dkv_ref[:, index * HEAD_SIZE : (index + 1) * HEAD_SIZE] = dvalue.astype(BF16)


def rows_spec(width):
    return pl.BlockSpec((MB_TOK, width), lambda i: (i, 0))


def same_spec(rows, width):
    return pl.BlockSpec((rows, width), lambda i: (0, 0))


def attend(q, kv, cosine, sine, position, q_gain, k_gain):
    tokens, q_width = q.shape
    kv_width = kv.shape[1]
    return pl.pallas_call(
        attend_kernel,
        grid=(tokens // MB_TOK,),
        in_specs=[rows_spec(q_width), rows_spec(kv_width)]
        + [rows_spec(HEAD_SIZE)] * 3
        + [same_spec(1, HEAD_SIZE)] * 2,
        out_specs=rows_spec(q_width),
        out_shape=jax.ShapeDtypeStruct((tokens, q_width), BF16),
        name="attend",
    )(q, kv, cosine, sine, position, q_gain, k_gain)


def attend_back(q, kv, cosine, sine, position, q_gain, k_gain, datt):
    tokens, q_width = q.shape
    kv_width = kv.shape[1]
    return pl.pallas_call(
        attend_back_kernel,
        grid=(tokens // MB_TOK,),
        in_specs=[rows_spec(q_width), rows_spec(kv_width)]
        + [rows_spec(HEAD_SIZE)] * 3
        + [same_spec(1, HEAD_SIZE)] * 2
        + [rows_spec(q_width)],
        out_specs=[
            rows_spec(q_width),
            rows_spec(kv_width),
            same_spec(8, HEAD_SIZE),
            same_spec(8, HEAD_SIZE),
        ],
        out_shape=[
            jax.ShapeDtypeStruct((tokens, q_width), BF16),
            jax.ShapeDtypeStruct((tokens, kv_width), BF16),
            jax.ShapeDtypeStruct((8, HEAD_SIZE), F32),
            jax.ShapeDtypeStruct((8, HEAD_SIZE), F32),
        ],
        name="attend_back",
    )(q, kv, cosine, sine, position, q_gain, k_gain, datt)


def rope_tables(position):
    half_width = HEAD_SIZE // 2
    frequency = ROPE_BASE ** (-2.0 * jnp.arange(half_width, dtype=F32) / HEAD_SIZE)
    angles = position[:, None] * frequency[None, :]
    cosine, sine = jnp.cos(angles), jnp.sin(angles)
    return (
        jnp.concatenate([cosine, cosine], axis=-1),
        jnp.concatenate([-sine, sine], axis=-1),
    )


def on_device(
    tokens_in,
    grad_out,
    seq_lengths,
    seq_deal,
    norm_attn,
    query_key_value_weight,
    query_norm_gain,
    k_gain,
    output_weight,
    norm_mlp,
    w_gate_up,
    w_down,
):
    place = Place()
    core = place.core
    tok_dev, width = tokens_in.shape
    query_width = QUERY_HEADS * HEAD_SIZE
    kv_width = KEY_VALUE_HEADS * HEAD_SIZE
    q_half, kv_half, out_half = query_width // 2, kv_width // 2, width // 2
    ff_block = w_down.shape[0]
    ff_half = ff_block * place.chips

    rows = query_key_value_weight.shape[0]

    def qkv_half(side):
        return jnp.concatenate(
            [
                lax.dynamic_slice_in_dim(query_key_value_weight, side * q_half, q_half, 1),
                lax.dynamic_slice_in_dim(
                    query_key_value_weight, query_width + side * kv_half, kv_half, 1
                ),
                lax.dynamic_slice_in_dim(
                    query_key_value_weight, query_width + kv_width + side * kv_half, kv_half, 1
                ),
            ],
            axis=1,
        )

    qkv_piece = ordered(core, qkv_half(core), swap_core(qkv_half(1 - core)), 0)
    out_piece = ordered(
        core,
        lax.dynamic_slice_in_dim(output_weight, core * out_half, out_half, 1),
        swap_core(lax.dynamic_slice_in_dim(output_weight, (1 - core) * out_half, out_half, 1)),
        0,
    )
    gate_split = w_gate_up.reshape(rows, 2, place.chips, 2, ff_block)
    gate_split = gate_split.transpose(3, 0, 1, 2, 4).reshape(2, rows, 2 * ff_half)
    gate_piece = ordered(core, pick(gate_split, core, 0), swap_core(pick(gate_split, 1 - core, 0)), 0)

    gain_rows, head_rows = norm_attn.shape[0], query_norm_gain.shape[0]
    small = jnp.concatenate([norm_attn, norm_mlp, query_norm_gain, k_gain])
    small_count = small.shape[0]
    small = jnp.pad(small, (0, -small_count % 128))[None, :]

    def own(values):
        return lax.dynamic_slice_in_dim(values, core * tok_dev, tok_dev, 0)

    def peer(values):
        return lax.dynamic_slice_in_dim(values, (1 - core) * tok_dev, tok_dev, 0)

    first_row = place.x * tok_dev
    own_rows = first_row + jnp.arange(tok_dev, dtype=jnp.int32)
    source, own_position = deal_rows(seq_lengths[0], seq_deal[0], own_rows)
    peer_tokens = swap_x(tokens_in)
    x_own = take_rows(tokens_in, peer_tokens, source, first_row).astype(BF16)
    x_low = ordered(core, x_own, swap_core(x_own), 0)
    own_position = own_position.astype(F32)
    position = ordered(core, own_position, swap_core(own_position), 0)
    grads_low = ordered(core, grad_out, swap_core(grad_out), 0)

    gains = gather_small(place, small)
    gain_one = gains[:, :gain_rows].reshape(1, width).astype(F32)
    gain_two = gains[:, gain_rows : 2 * gain_rows].reshape(1, width).astype(F32)
    gain_q = gains[:, 2 * gain_rows : 2 * gain_rows + head_rows].reshape(1, HEAD_SIZE).astype(F32)
    gain_k = gains[:, 2 * gain_rows + head_rows : small_count].reshape(1, HEAD_SIZE).astype(F32)

    w_q, w_kv = gather_halves(place, qkv_piece)
    w_out_a, w_out_b = gather_halves(place, out_piece)
    w_gate, w_up = gather_halves(place, gate_piece)
    w_low = gather_late_z(place, w_down)
    w_out = jnp.concatenate([w_out_a, w_out_b], axis=1)

    cosine, sine = rope_tables(position)
    position_wide = jnp.broadcast_to(position.astype(jnp.int32)[:, None], (2 * tok_dev, MB_TOK))

    x = x_low.astype(F32)
    scale_one = row_scale(x)
    normed_one = (x * scale_one * gain_one).astype(BF16)
    q = jnp.dot(normed_one, w_q, preferred_element_type=F32)
    kv = jnp.dot(normed_one, w_kv, preferred_element_type=F32)
    att = attend(q, kv, cosine, sine, position_wide, gain_q, gain_k)
    att_peer = swap_core(att)
    w_out_own = lax.dynamic_slice_in_dim(w_out, core * q_half, q_half, 0)
    w_out_peer = lax.dynamic_slice_in_dim(w_out, (1 - core) * q_half, q_half, 0)
    delta = (
        jnp.dot(att, w_out_own, preferred_element_type=F32)
        + jnp.dot(att_peer, w_out_peer, preferred_element_type=F32)
    ).astype(BF16)
    residual = x + ordered(core, delta, swap_core(delta), 1).astype(F32)
    scale_two = row_scale(residual)
    normed_two = (residual * scale_two * gain_two).astype(BF16)
    gate = jnp.dot(normed_two, w_gate, preferred_element_type=F32)
    up = jnp.dot(normed_two, w_up, preferred_element_type=F32)
    sigmoid = jax.nn.sigmoid(gate)
    activated = (gate * sigmoid * up).astype(BF16)
    down = jnp.dot(activated, w_low, preferred_element_type=F32)
    y_out = (
        own(residual) + own(down) + swap_core(peer(down).astype(BF16)).astype(F32)
    ).astype(BF16)

    term_down = t_dot(activated, grads_low).astype(BF16)
    out_down = scatter_late_xy(place, term_down)
    grad_act = dot_t(grads_low, w_low)
    grad_gate = (grad_act * up * (sigmoid * (1.0 + gate * (1.0 - sigmoid)))).astype(BF16)
    grad_up = (grad_act * (gate * sigmoid)).astype(BF16)
    term_gate = t_dot(normed_two, grad_gate).astype(BF16)
    term_up = t_dot(normed_two, grad_up).astype(BF16)
    out_gate = scatter_halves(place, term_gate, term_up)
    part_two = dot_t(grad_gate, w_gate) + dot_t(grad_up, w_up)
    grad_normed_two = part_two + swap_core(part_two.astype(BF16)).astype(F32)
    term_norm_two = jnp.sum(own(grad_normed_two * residual * scale_two), axis=0)
    grad_residual = grads_low.astype(F32) + norm_back(
        grad_normed_two, residual, scale_two, gain_two
    )
    branch = grad_residual.astype(BF16)
    branch_own = lax.dynamic_slice_in_dim(branch, core * out_half, out_half, 1)
    datt = (
        dot_t(branch_own, w_out_own)
        + swap_core(dot_t(branch_own, w_out_peer).astype(BF16)).astype(F32)
    ).astype(BF16)
    term_out_own = t_dot(att, branch_own).astype(BF16)
    term_out_peer = t_dot(att_peer, branch_own).astype(BF16)
    term_out = ordered(core, term_out_own, term_out_peer, 0)
    out_quarter = out_half // 2
    out_out = scatter_halves(place, term_out[:, :out_quarter], term_out[:, out_quarter:])
    dq, dkv, sum_q, sum_k = attend_back(
        q, kv, cosine, sine, position_wide, gain_q, gain_k, datt
    )
    term_q = t_dot(normed_one, dq).astype(BF16)
    term_kv = t_dot(normed_one, dkv).astype(BF16)
    out_qkv = scatter_halves(place, term_q, term_kv)
    part_one = dot_t(dq, w_q) + dot_t(dkv, w_kv)
    grad_normed_one = own(part_one) + swap_core(peer(part_one).astype(BF16)).astype(F32)
    x_first, scale_first = own(x), own(scale_one)
    term_norm_one = jnp.sum(grad_normed_one * x_first * scale_first, axis=0)
    grad_dealt = (
        own(grad_residual) + norm_back(grad_normed_one, x_first, scale_first, gain_one)
    ).astype(BF16)
    target = back_rows(seq_lengths[0], seq_deal[0], own_rows)
    grad_in = take_rows(grad_dealt, swap_x(grad_dealt), target, first_row)

    def unsplit(chip_rows, device_rows):
        chip_rows = chip_rows.reshape(2, device_rows, chip_rows.shape[1])
        return paired(core, pick(chip_rows, core, 0), swap_core(pick(chip_rows, 1 - core, 0)), 1)

    both = unsplit(out_qkv, rows)
    grad_qkv = jnp.concatenate(
        [
            both[:, :, :q_half].reshape(rows, query_width),
            both[:, :, q_half : q_half + kv_half].reshape(rows, kv_width),
            both[:, :, q_half + kv_half :].reshape(rows, kv_width),
        ],
        axis=1,
    )
    grad_out_proj = unsplit(out_out, output_weight.shape[0]).reshape(output_weight.shape)
    both = unsplit(out_gate, rows)
    grad_gate_up = (
        both.reshape(rows, 2, 2, place.chips, ff_block)
        .transpose(0, 2, 3, 1, 4)
        .reshape(rows, w_gate_up.shape[1])
    )

    devices = 2 * place.chips
    sums = jnp.concatenate(
        [
            term_norm_one.reshape(devices, gain_rows),
            term_norm_two.reshape(devices, gain_rows),
            jnp.sum(sum_q, axis=0).reshape(devices, head_rows),
            jnp.sum(sum_k, axis=0).reshape(devices, head_rows),
        ],
        axis=1,
    )
    sums = jnp.pad(sums, ((0, 0), (0, -small_count % 128)))
    owned = scatter_small(place, sums)
    return (
        y_out,
        grad_in,
        owned[:gain_rows],
        grad_qkv,
        owned[2 * gain_rows : 2 * gain_rows + head_rows],
        owned[2 * gain_rows + head_rows : small_count],
        grad_out_proj,
        owned[gain_rows : 2 * gain_rows],
        grad_gate_up,
        out_down,
    )


def norm_back(grad_norm, inputs, scale, gain):
    weighted = grad_norm * gain
    return scale * weighted - inputs * (scale * scale * scale) * jnp.mean(
        weighted * inputs, axis=-1, keepdims=True
    )


def scatter_late_xy(place, grads):
    depth = place.depth
    rows, cols = grads.shape[0] // (4 * depth), grads.shape[1]
    half = cols // 2
    grads = grads.reshape(2, depth, 2, rows, cols)
    total = pick(grads, place.z, 1).astype(F32)
    for step in range(1, depth):
        total = total + swap_z(pick(grads, place.z ^ step, 1), step).astype(F32)
    total = total.astype(BF16)
    first, second = total[..., :half], total[..., half:]
    first = add(pick(first, place.y, 1), swap_y(pick(first, 1 - place.y, 1)))
    first = pick(first, place.x, 0).astype(F32) + swap_x(pick(first, 1 - place.x, 0)).astype(F32)
    second = add(pick(second, place.x, 0), swap_x(pick(second, 1 - place.x, 0)))
    second = pick(second, place.y, 0).astype(F32) + swap_y(pick(second, 1 - place.y, 0)).astype(
        F32
    )
    return jnp.concatenate([first, second], axis=1)


def solution(mesh):
    rows = P(("grp", "dp"), None)
    line = P(("grp", "dp"))
    return jax.shard_map(
        on_device,
        mesh=mesh,
        in_specs=(rows, rows, P("dp", None), P("dp", None), line, rows, line, line, rows, line, rows, rows),
        out_specs=(rows, rows, line, rows, line, line, rows, line, rows, rows),
        check_vma=False,
    )
```

```python
import jax
import jax.numpy as jnp
from jax import lax
from jax.experimental import pallas as pl
from jax.experimental.pallas import tpu as pltpu
from jax.sharding import PartitionSpec as P

QUERY_HEADS = 16
KEY_VALUE_HEADS = 8
HEAD_SIZE = 128
FF = 3072
MB_TOK = 128
SEQ_GROUP = 4

EPSILON = 1e-06
ROPE_BASE = 1000000.0
MASKED = -1e30
SCALE = HEAD_SIZE**-0.5
QUERIES_PER_KEY = QUERY_HEADS // KEY_VALUE_HEADS

BF16 = jnp.bfloat16
F32 = jnp.float32


def deal_slots(lengths, deal_order):
    token_count = lengths.shape[0]
    seq_ids = jnp.arange(token_count, dtype=jnp.int32)
    starts = jnp.cumsum(lengths) - lengths
    pick = (deal_order[:, None] == seq_ids[None, :]).astype(jnp.int32)
    slot_length = jnp.sum(pick * lengths[None, :], axis=1)
    slot_source = jnp.sum(pick * starts[None, :], axis=1)
    groups = token_count // SEQ_GROUP
    grouped = slot_length.reshape(groups, SEQ_GROUP)
    offsets = jnp.cumsum(grouped, axis=1) - grouped
    slot_dealt = (offsets + jnp.arange(groups, dtype=jnp.int32)[:, None] * MB_TOK).reshape(
        token_count
    )
    return (seq_ids, starts, pick, slot_length, slot_source, slot_dealt)


def deal_rows(lengths, deal_order, rows):
    _, _, _, slot_length, slot_source, slot_dealt = deal_slots(lengths, deal_order)
    inside = (
        (rows[:, None] >= slot_dealt[None, :])
        & (rows[:, None] < (slot_dealt + slot_length)[None, :])
    ).astype(jnp.int32)
    source = rows + jnp.sum(inside * (slot_source - slot_dealt)[None, :], axis=1)
    position = rows - jnp.sum(inside * slot_dealt[None, :], axis=1)
    return (source, position)


def back_rows(lengths, deal_order, rows):
    _, starts, pick, _, _, slot_dealt = deal_slots(lengths, deal_order)
    seq_dealt = jnp.sum(pick * slot_dealt[:, None], axis=0)
    inside = (
        (rows[:, None] >= starts[None, :]) & (rows[:, None] < (starts + lengths)[None, :])
    ).astype(jnp.int32)
    return rows + jnp.sum(inside * (seq_dealt - starts)[None, :], axis=1)


def take_rows(own, peer, rows, first_row):
    half = own.shape[0]
    near = jnp.remainder(rows - first_row, 2 * half)
    lane = lax.broadcasted_iota(jnp.int32, (rows.shape[0], half), 1)
    pick_own = (near[:, None] == lane).astype(own.dtype)
    pick_peer = (near[:, None] == lane + half).astype(own.dtype)
    return jnp.dot(pick_own, own, preferred_element_type=F32) + jnp.dot(
        pick_peer, peer, preferred_element_type=F32
    )


CHIPS = ("x", "z", "y")
DEVICES = ("x", "z", "y", "core")


def swap(values, axis, mask):
    size = lax.axis_size(axis)
    return lax.ppermute(values, axis, [(i, i ^ mask) for i in range(size)])


def swap_core(values):
    return swap(values, "core", 1)


def swap_y(values):
    return swap(values, "y", 1)


def swap_z(values, step):
    return swap(values, "z", step)


def swap_x(values):
    return swap(values, "x", 1)


class Place:
    def __init__(self):
        self.x = lax.axis_index("x")
        self.core = lax.axis_index("core")
        self.y = lax.axis_index("y")
        self.z = lax.axis_index("z")
        self.depth = lax.axis_size("z")
        self.chips = 4 * self.depth


def ordered(bit, own, peer, axis):
    return jnp.where(
        bit == 0,
        jnp.concatenate([own, peer], axis=axis),
        jnp.concatenate([peer, own], axis=axis),
    )


def pick(values, index, axis):
    return lax.dynamic_index_in_dim(values, index, axis, keepdims=False)


def paired(bit, own, peer, axis):
    return ordered(bit, jnp.expand_dims(own, axis), jnp.expand_dims(peer, axis), axis)


def by_z(place, pieces, axis):
    step = 1
    groups = [jnp.expand_dims(piece, axis) for piece in pieces]
    while step < place.depth:
        bit = (place.z // step) % 2
        groups = [
            ordered(bit, groups[2 * i], groups[2 * i + 1], axis) for i in range(len(groups) // 2)
        ]
        step *= 2
    return groups[0]


def spread_z(place, piece, axis):
    pieces = [piece] + [swap_z(piece, step) for step in range(1, place.depth)]
    return by_z(place, pieces, axis)


def gather_late_x(place, stack):
    stack = paired(place.y, stack, swap_y(stack), 1)
    stack = paired(place.x, stack, swap_x(stack), 0)
    return stack.reshape(-1, stack.shape[-1])


def gather_late_y(place, stack):
    stack = paired(place.x, stack, swap_x(stack), 0)
    stack = paired(place.y, stack, swap_y(stack), 2)
    return stack.reshape(-1, stack.shape[-1])


def gather_halves(place, piece):
    half = piece.shape[1] // 2
    stack = spread_z(place, piece, 0)
    return (
        gather_late_x(place, stack[..., :half]),
        gather_late_y(place, stack[..., half:]),
    )


def add(first, second):
    return (first.astype(F32) + second.astype(F32)).astype(BF16)


def scatter_plane(place, grads, first):
    depth = place.depth
    rows = grads.shape[0] // (4 * depth)
    grads = grads.reshape(2, depth, 2, rows, grads.shape[1])
    if first == "x":
        part = add(pick(grads, place.x, 0), swap_x(pick(grads, 1 - place.x, 0)))
        return add(pick(part, place.y, 1), swap_y(pick(part, 1 - place.y, 1)))
    part = add(pick(grads, place.y, 2), swap_y(pick(grads, 1 - place.y, 2)))
    return add(pick(part, place.x, 0), swap_x(pick(part, 1 - place.x, 0)))


def scatter_z(place, part):
    total = pick(part, place.z, 0).astype(F32)
    for step in range(1, place.depth):
        total = total + swap_z(pick(part, place.z ^ step, 0), step).astype(F32)
    return total


def scatter_halves(place, grads_a, grads_b):
    part = jnp.concatenate(
        [scatter_plane(place, grads_a, "x"), scatter_plane(place, grads_b, "y")], axis=-1
    )
    return scatter_z(place, part)


def gather_small(place, row):
    stack = ordered(place.core, row, swap_core(row), 0)
    stack = spread_z(place, stack, 0)
    stack = paired(place.y, stack, swap_y(stack), 1)
    stack = paired(place.x, stack, swap_x(stack), 0)
    return stack.reshape(-1, row.shape[1])


def scatter_small(place, rows):
    grads = rows.reshape(2, place.depth, 2, 2, rows.shape[1])
    grads = pick(grads, place.core, 3) + swap_core(pick(grads, 1 - place.core, 3))
    grads = pick(grads, place.x, 0) + swap_x(pick(grads, 1 - place.x, 0))
    grads = pick(grads, place.y, 1) + swap_y(pick(grads, 1 - place.y, 1))
    total = pick(grads, place.z, 0)
    for step in range(1, place.depth):
        total = total + swap_z(pick(grads, place.z ^ step, 0), step)
    return total


def rope(values, cosine, sine):
    return values * cosine + pltpu.roll(values, HEAD_SIZE // 2, 1) * sine


def rope_back(grads, cosine, sine):
    return grads * cosine + pltpu.roll(grads * sine, HEAD_SIZE // 2, 1)


def row_scale(values):
    return lax.rsqrt(jnp.mean(values * values, axis=-1, keepdims=True) + EPSILON)


def head(ref, index):
    return ref[:, index * HEAD_SIZE : (index + 1) * HEAD_SIZE]


def dot_t(left, right):
    return lax.dot_general(left, right, (((1,), (1,)), ((), ())), preferred_element_type=F32)


def t_dot(left, right):
    return lax.dot_general(left, right, (((0,), (0,)), ((), ())), preferred_element_type=F32)


def allowed_keys(position):
    row = lax.broadcasted_iota(jnp.int32, (MB_TOK, MB_TOK), 0)
    key = lax.broadcasted_iota(jnp.int32, (MB_TOK, MB_TOK), 1)
    allowed = (key <= row) & (key >= row - position)
    return jnp.concatenate([allowed] * QUERIES_PER_KEY, axis=0)


def attend_kernel(q_ref, kv_ref, cos_ref, sin_ref, pos_ref, qg_ref, kg_ref, out_ref):
    heads = kv_ref.shape[1] // (2 * HEAD_SIZE)
    cosine, sine = cos_ref[...], sin_ref[...]
    allowed = allowed_keys(pos_ref[...])
    for j in range(heads):
        keys = head(kv_ref, j)
        key_low = rope(keys * row_scale(keys) * kg_ref[...], cosine, sine).astype(BF16)
        value = head(kv_ref, heads + j).astype(BF16)
        queries = []
        for g in range(QUERIES_PER_KEY):
            query = head(q_ref, QUERIES_PER_KEY * j + g)
            queries.append(
                rope(query * row_scale(query) * qg_ref[...], cosine, sine).astype(BF16)
            )
        scores = dot_t(jnp.concatenate(queries, axis=0), key_low) * SCALE
        scores = jnp.where(allowed, scores, MASKED)
        expo = jnp.exp(scores - jnp.max(scores, axis=-1, keepdims=True))
        probs = (expo / jnp.sum(expo, axis=-1, keepdims=True)).astype(BF16)
        mixed = jnp.dot(probs, value, preferred_element_type=F32).astype(BF16)
        for g in range(QUERIES_PER_KEY):
            index = QUERIES_PER_KEY * j + g
            out_ref[:, index * HEAD_SIZE : (index + 1) * HEAD_SIZE] = mixed[
                g * MB_TOK : (g + 1) * MB_TOK
            ]


def attend_back_kernel(
    q_ref, kv_ref, cos_ref, sin_ref, pos_ref, qg_ref, kg_ref, datt_ref,
    dq_ref, dkv_ref, sum_q_ref, sum_k_ref,
):
    heads = kv_ref.shape[1] // (2 * HEAD_SIZE)
    cosine, sine = cos_ref[...], sin_ref[...]
    allowed = allowed_keys(pos_ref[...])

    @pl.when(pl.program_id(0) == 0)
    def _():
        sum_q_ref[...] = jnp.zeros_like(sum_q_ref)
        sum_k_ref[...] = jnp.zeros_like(sum_k_ref)

    def normed_back(grad_low, raw, scale, gain):
        grad = rope_back(grad_low, cosine, sine)
        term = jnp.sum((grad * raw * scale).reshape(-1, 8, HEAD_SIZE), axis=0)
        weighted = grad * gain
        back = scale * weighted - raw * (scale * scale * scale) * jnp.mean(
            weighted * raw, axis=-1, keepdims=True
        )
        return back, term

    for j in range(heads):
        keys = head(kv_ref, j)
        key_scale = row_scale(keys)
        key_low = rope(keys * key_scale * kg_ref[...], cosine, sine).astype(BF16)
        value = head(kv_ref, heads + j).astype(BF16)
        raws, scales, lows, datts = [], [], [], []
        for g in range(QUERIES_PER_KEY):
            query = head(q_ref, QUERIES_PER_KEY * j + g)
            scale = row_scale(query)
            raws.append(query)
            scales.append(scale)
            lows.append(rope(query * scale * qg_ref[...], cosine, sine).astype(BF16))
            datts.append(head(datt_ref, QUERIES_PER_KEY * j + g))
        low = jnp.concatenate(lows, axis=0)
        datt = jnp.concatenate(datts, axis=0)
        scores = jnp.where(allowed, dot_t(low, key_low) * SCALE, MASKED)
        expo = jnp.exp(scores - jnp.max(scores, axis=-1, keepdims=True))
        probs = expo / jnp.sum(expo, axis=-1, keepdims=True)
        dprobs = dot_t(datt, value)
        dscores = (
            probs * (dprobs - jnp.sum(probs * dprobs, axis=-1, keepdims=True))
        ).astype(BF16)
        dlow = jnp.dot(dscores, key_low, preferred_element_type=F32) * SCALE
        dkey = t_dot(dscores, low) * SCALE
        dvalue = t_dot(probs.astype(BF16), datt)
        for g in range(QUERIES_PER_KEY):
            index = QUERIES_PER_KEY * j + g
            back, term = normed_back(
                dlow[g * MB_TOK : (g + 1) * MB_TOK], raws[g], scales[g], qg_ref[...]
            )
            dq_ref[:, index * HEAD_SIZE : (index + 1) * HEAD_SIZE] = back.astype(BF16)
            sum_q_ref[...] += term
        back, term = normed_back(dkey, keys, key_scale, kg_ref[...])
        dkv_ref[:, j * HEAD_SIZE : (j + 1) * HEAD_SIZE] = back.astype(BF16)
        sum_k_ref[...] += term
        index = heads + j
        dkv_ref[:, index * HEAD_SIZE : (index + 1) * HEAD_SIZE] = dvalue.astype(BF16)


def rows_spec(width):
    return pl.BlockSpec((MB_TOK, width), lambda i: (i, 0))


def same_spec(rows, width):
    return pl.BlockSpec((rows, width), lambda i: (0, 0))


def attend(q, kv, cosine, sine, position, q_gain, k_gain):
    tokens, q_width = q.shape
    kv_width = kv.shape[1]
    return pl.pallas_call(
        attend_kernel,
        grid=(tokens // MB_TOK,),
        in_specs=[rows_spec(q_width), rows_spec(kv_width)]
        + [rows_spec(HEAD_SIZE)] * 3
        + [same_spec(1, HEAD_SIZE)] * 2,
        out_specs=rows_spec(q_width),
        out_shape=jax.ShapeDtypeStruct((tokens, q_width), BF16),
        name="attend",
    )(q, kv, cosine, sine, position, q_gain, k_gain)


def attend_back(q, kv, cosine, sine, position, q_gain, k_gain, datt):
    tokens, q_width = q.shape
    kv_width = kv.shape[1]
    return pl.pallas_call(
        attend_back_kernel,
        grid=(tokens // MB_TOK,),
        in_specs=[rows_spec(q_width), rows_spec(kv_width)]
        + [rows_spec(HEAD_SIZE)] * 3
        + [same_spec(1, HEAD_SIZE)] * 2
        + [rows_spec(q_width)],
        out_specs=[
            rows_spec(q_width),
            rows_spec(kv_width),
            same_spec(8, HEAD_SIZE),
            same_spec(8, HEAD_SIZE),
        ],
        out_shape=[
            jax.ShapeDtypeStruct((tokens, q_width), BF16),
            jax.ShapeDtypeStruct((tokens, kv_width), BF16),
            jax.ShapeDtypeStruct((8, HEAD_SIZE), F32),
            jax.ShapeDtypeStruct((8, HEAD_SIZE), F32),
        ],
        name="attend_back",
    )(q, kv, cosine, sine, position, q_gain, k_gain, datt)


def rope_tables(position):
    half_width = HEAD_SIZE // 2
    frequency = ROPE_BASE ** (-2.0 * jnp.arange(half_width, dtype=F32) / HEAD_SIZE)
    angles = position[:, None] * frequency[None, :]
    cosine, sine = jnp.cos(angles), jnp.sin(angles)
    return (
        jnp.concatenate([cosine, cosine], axis=-1),
        jnp.concatenate([-sine, sine], axis=-1),
    )


def on_device(
    tokens_in,
    grad_out,
    seq_lengths,
    seq_deal,
    norm_attn,
    query_key_value_weight,
    query_norm_gain,
    k_gain,
    output_weight,
    norm_mlp,
    w_gate_up,
    w_down,
):
    place = Place()
    core = place.core
    tok_dev, width = tokens_in.shape
    query_width = QUERY_HEADS * HEAD_SIZE
    kv_width = KEY_VALUE_HEADS * HEAD_SIZE
    q_half, kv_half, out_half = query_width // 2, kv_width // 2, width // 2
    ff_block = w_down.shape[0]
    ff_half = ff_block * place.chips

    rows = query_key_value_weight.shape[0]

    def qkv_half(side):
        return jnp.concatenate(
            [
                lax.dynamic_slice_in_dim(query_key_value_weight, side * q_half, q_half, 1),
                lax.dynamic_slice_in_dim(
                    query_key_value_weight, query_width + side * kv_half, kv_half, 1
                ),
                lax.dynamic_slice_in_dim(
                    query_key_value_weight, query_width + kv_width + side * kv_half, kv_half, 1
                ),
            ],
            axis=1,
        )

    qkv_piece = ordered(core, qkv_half(core), swap_core(qkv_half(1 - core)), 0)
    out_piece = ordered(
        core,
        lax.dynamic_slice_in_dim(output_weight, core * out_half, out_half, 1),
        swap_core(lax.dynamic_slice_in_dim(output_weight, (1 - core) * out_half, out_half, 1)),
        0,
    )
    gate_split = w_gate_up.reshape(rows, 2, place.chips, 2, ff_block)
    gate_split = gate_split.transpose(3, 0, 1, 2, 4).reshape(2, rows, 2 * ff_half)
    gate_piece = ordered(core, pick(gate_split, core, 0), swap_core(pick(gate_split, 1 - core, 0)), 0)

    gain_rows, head_rows = norm_attn.shape[0], query_norm_gain.shape[0]
    small = jnp.concatenate([norm_attn, norm_mlp, query_norm_gain, k_gain])
    small_count = small.shape[0]
    small = jnp.pad(small, (0, -small_count % 128))[None, :]

    def own(values):
        return lax.dynamic_slice_in_dim(values, core * tok_dev, tok_dev, 0)

    def peer(values):
        return lax.dynamic_slice_in_dim(values, (1 - core) * tok_dev, tok_dev, 0)

    first_row = place.x * tok_dev
    own_rows = first_row + jnp.arange(tok_dev, dtype=jnp.int32)
    source, own_position = deal_rows(seq_lengths[0], seq_deal[0], own_rows)
    peer_tokens = swap_x(tokens_in)
    x_own = take_rows(tokens_in, peer_tokens, source, first_row).astype(BF16)
    x_low = ordered(core, x_own, swap_core(x_own), 0)
    own_position = own_position.astype(F32)
    position = ordered(core, own_position, swap_core(own_position), 0)
    grads_low = ordered(core, grad_out, swap_core(grad_out), 0)

    gains = gather_small(place, small)
    gain_one = gains[:, :gain_rows].reshape(1, width).astype(F32)
    gain_two = gains[:, gain_rows : 2 * gain_rows].reshape(1, width).astype(F32)
    gain_q = gains[:, 2 * gain_rows : 2 * gain_rows + head_rows].reshape(1, HEAD_SIZE).astype(F32)
    gain_k = gains[:, 2 * gain_rows + head_rows : small_count].reshape(1, HEAD_SIZE).astype(F32)

    w_q, w_kv = gather_halves(place, qkv_piece)
    w_out_a, w_out_b = gather_halves(place, out_piece)
    w_gate, w_up = gather_halves(place, gate_piece)
    w_low = lax.all_gather(w_down, CHIPS, axis=0, tiled=True)
    w_out = jnp.concatenate([w_out_a, w_out_b], axis=1)

    cosine, sine = rope_tables(position)
    position_wide = jnp.broadcast_to(position.astype(jnp.int32)[:, None], (2 * tok_dev, MB_TOK))

    x = x_low.astype(F32)
    scale_one = row_scale(x)
    normed_one = (x * scale_one * gain_one).astype(BF16)
    q = jnp.dot(normed_one, w_q, preferred_element_type=F32)
    kv = jnp.dot(normed_one, w_kv, preferred_element_type=F32)
    att = attend(q, kv, cosine, sine, position_wide, gain_q, gain_k)
    att_peer = swap_core(att)
    w_out_own = lax.dynamic_slice_in_dim(w_out, core * q_half, q_half, 0)
    w_out_peer = lax.dynamic_slice_in_dim(w_out, (1 - core) * q_half, q_half, 0)
    delta = (
        jnp.dot(att, w_out_own, preferred_element_type=F32)
        + jnp.dot(att_peer, w_out_peer, preferred_element_type=F32)
    ).astype(BF16)
    residual = x + ordered(core, delta, swap_core(delta), 1).astype(F32)
    scale_two = row_scale(residual)
    normed_two = (residual * scale_two * gain_two).astype(BF16)
    gate = jnp.dot(normed_two, w_gate, preferred_element_type=F32)
    up = jnp.dot(normed_two, w_up, preferred_element_type=F32)
    sigmoid = jax.nn.sigmoid(gate)
    activated = (gate * sigmoid * up).astype(BF16)
    down = jnp.dot(activated, w_low, preferred_element_type=F32)
    y_out = (
        own(residual) + own(down) + swap_core(peer(down).astype(BF16)).astype(F32)
    ).astype(BF16)

    term_down = t_dot(activated, grads_low).astype(BF16)
    out_down = lax.psum_scatter(term_down, CHIPS, scatter_dimension=0, tiled=True).astype(F32)
    grad_act = dot_t(grads_low, w_low)
    grad_gate = (grad_act * up * (sigmoid * (1.0 + gate * (1.0 - sigmoid)))).astype(BF16)
    grad_up = (grad_act * (gate * sigmoid)).astype(BF16)
    term_gate = t_dot(normed_two, grad_gate).astype(BF16)
    term_up = t_dot(normed_two, grad_up).astype(BF16)
    out_gate = scatter_halves(place, term_gate, term_up)
    part_two = dot_t(grad_gate, w_gate) + dot_t(grad_up, w_up)
    grad_normed_two = part_two + swap_core(part_two.astype(BF16)).astype(F32)
    term_norm_two = jnp.sum(own(grad_normed_two * residual * scale_two), axis=0)
    grad_residual = grads_low.astype(F32) + norm_back(
        grad_normed_two, residual, scale_two, gain_two
    )
    branch = grad_residual.astype(BF16)
    branch_own = lax.dynamic_slice_in_dim(branch, core * out_half, out_half, 1)
    datt = (
        dot_t(branch_own, w_out_own)
        + swap_core(dot_t(branch_own, w_out_peer).astype(BF16)).astype(F32)
    ).astype(BF16)
    term_out_own = t_dot(att, branch_own).astype(BF16)
    term_out_peer = t_dot(att_peer, branch_own).astype(BF16)
    term_out = ordered(core, term_out_own, term_out_peer, 0)
    out_quarter = out_half // 2
    out_out = scatter_halves(place, term_out[:, :out_quarter], term_out[:, out_quarter:])
    dq, dkv, sum_q, sum_k = attend_back(
        q, kv, cosine, sine, position_wide, gain_q, gain_k, datt
    )
    term_q = t_dot(normed_one, dq).astype(BF16)
    term_kv = t_dot(normed_one, dkv).astype(BF16)
    out_qkv = scatter_halves(place, term_q, term_kv)
    part_one = dot_t(dq, w_q) + dot_t(dkv, w_kv)
    grad_normed_one = own(part_one) + swap_core(peer(part_one).astype(BF16)).astype(F32)
    x_first, scale_first = own(x), own(scale_one)
    term_norm_one = jnp.sum(grad_normed_one * x_first * scale_first, axis=0)
    grad_dealt = (
        own(grad_residual) + norm_back(grad_normed_one, x_first, scale_first, gain_one)
    ).astype(BF16)
    target = back_rows(seq_lengths[0], seq_deal[0], own_rows)
    grad_in = take_rows(grad_dealt, swap_x(grad_dealt), target, first_row)

    def unsplit(chip_rows, device_rows):
        chip_rows = chip_rows.reshape(2, device_rows, chip_rows.shape[1])
        return paired(core, pick(chip_rows, core, 0), swap_core(pick(chip_rows, 1 - core, 0)), 1)

    both = unsplit(out_qkv, rows)
    grad_qkv = jnp.concatenate(
        [
            both[:, :, :q_half].reshape(rows, query_width),
            both[:, :, q_half : q_half + kv_half].reshape(rows, kv_width),
            both[:, :, q_half + kv_half :].reshape(rows, kv_width),
        ],
        axis=1,
    )
    grad_out_proj = unsplit(out_out, output_weight.shape[0]).reshape(output_weight.shape)
    both = unsplit(out_gate, rows)
    grad_gate_up = (
        both.reshape(rows, 2, 2, place.chips, ff_block)
        .transpose(0, 2, 3, 1, 4)
        .reshape(rows, w_gate_up.shape[1])
    )

    devices = 2 * place.chips
    sums = jnp.concatenate(
        [
            term_norm_one.reshape(devices, gain_rows),
            term_norm_two.reshape(devices, gain_rows),
            jnp.sum(sum_q, axis=0).reshape(devices, head_rows),
            jnp.sum(sum_k, axis=0).reshape(devices, head_rows),
        ],
        axis=1,
    )
    sums = jnp.pad(sums, ((0, 0), (0, -small_count % 128)))
    owned = scatter_small(place, sums)
    return (
        y_out,
        grad_in,
        owned[:gain_rows],
        grad_qkv,
        owned[2 * gain_rows : 2 * gain_rows + head_rows],
        owned[2 * gain_rows + head_rows : small_count],
        grad_out_proj,
        owned[gain_rows : 2 * gain_rows],
        grad_gate_up,
        out_down,
    )


def norm_back(grad_norm, inputs, scale, gain):
    weighted = grad_norm * gain
    return scale * weighted - inputs * (scale * scale * scale) * jnp.mean(
        weighted * inputs, axis=-1, keepdims=True
    )


def solution(mesh):
    groups, size = mesh.shape["grp"], mesh.shape["dp"]
    mesh = jax.sharding.Mesh(mesh.devices.reshape(groups, size // 4, 2, 2), DEVICES)
    rows, line, pairs = P(DEVICES, None), P(DEVICES), P(("z", "y", "core"), None)
    return jax.shard_map(
        on_device,
        mesh=mesh,
        in_specs=(rows, rows, pairs, pairs, line, rows, line, line, rows, line, rows, rows),
        out_specs=(rows, rows, line, rows, line, line, rows, line, rows, rows),
        check_vma=False,
    )
```

```python
import jax
import jax.numpy as jnp
from jax import lax
from jax.experimental import pallas as pl
from jax.experimental.pallas import tpu as pltpu
from jax.sharding import PartitionSpec as P

QUERY_HEADS = 16
KEY_VALUE_HEADS = 8
HEAD_SIZE = 128
FF = 3072
MB_TOK = 128
SEQ_GROUP = 4

EPSILON = 1e-06
ROPE_BASE = 1000000.0
MASKED = -1e30
SCALE = HEAD_SIZE**-0.5
QUERIES_PER_KEY = QUERY_HEADS // KEY_VALUE_HEADS

BF16 = jnp.bfloat16
F32 = jnp.float32


def deal_slots(lengths, deal_order):
    token_count = lengths.shape[0]
    seq_ids = jnp.arange(token_count, dtype=jnp.int32)
    starts = jnp.cumsum(lengths) - lengths
    pick = (deal_order[:, None] == seq_ids[None, :]).astype(jnp.int32)
    slot_length = jnp.sum(pick * lengths[None, :], axis=1)
    slot_source = jnp.sum(pick * starts[None, :], axis=1)
    groups = token_count // SEQ_GROUP
    grouped = slot_length.reshape(groups, SEQ_GROUP)
    offsets = jnp.cumsum(grouped, axis=1) - grouped
    slot_dealt = (offsets + jnp.arange(groups, dtype=jnp.int32)[:, None] * MB_TOK).reshape(
        token_count
    )
    return (seq_ids, starts, pick, slot_length, slot_source, slot_dealt)


def deal_rows(lengths, deal_order, rows):
    _, _, _, slot_length, slot_source, slot_dealt = deal_slots(lengths, deal_order)
    inside = (
        (rows[:, None] >= slot_dealt[None, :])
        & (rows[:, None] < (slot_dealt + slot_length)[None, :])
    ).astype(jnp.int32)
    source = rows + jnp.sum(inside * (slot_source - slot_dealt)[None, :], axis=1)
    position = rows - jnp.sum(inside * slot_dealt[None, :], axis=1)
    return (source, position)


def back_rows(lengths, deal_order, rows):
    _, starts, pick, _, _, slot_dealt = deal_slots(lengths, deal_order)
    seq_dealt = jnp.sum(pick * slot_dealt[:, None], axis=0)
    inside = (
        (rows[:, None] >= starts[None, :]) & (rows[:, None] < (starts + lengths)[None, :])
    ).astype(jnp.int32)
    return rows + jnp.sum(inside * (seq_dealt - starts)[None, :], axis=1)


def take_rows(own, peer, rows, first_row):
    half = own.shape[0]
    near = jnp.remainder(rows - first_row, 2 * half)
    lane = lax.broadcasted_iota(jnp.int32, (rows.shape[0], half), 1)
    pick_own = (near[:, None] == lane).astype(own.dtype)
    pick_peer = (near[:, None] == lane + half).astype(own.dtype)
    return jnp.dot(pick_own, own, preferred_element_type=F32) + jnp.dot(
        pick_peer, peer, preferred_element_type=F32
    )


CHIPS = ("x", "z", "y")
DEVICES = ("x", "z", "y", "core")


def swap(values, axis, mask):
    size = lax.axis_size(axis)
    return lax.ppermute(values, axis, [(i, i ^ mask) for i in range(size)])


def swap_core(values):
    return swap(values, "core", 1)


def swap_y(values):
    return swap(values, "y", 1)


def swap_z(values, step):
    return swap(values, "z", step)


def swap_x(values):
    return swap(values, "x", 1)


class Place:
    def __init__(self):
        self.x = lax.axis_index("x")
        self.core = lax.axis_index("core")
        self.y = lax.axis_index("y")
        self.z = lax.axis_index("z")
        self.depth = lax.axis_size("z")
        self.chips = 4 * self.depth


def ordered(bit, own, peer, axis):
    return jnp.where(
        bit == 0,
        jnp.concatenate([own, peer], axis=axis),
        jnp.concatenate([peer, own], axis=axis),
    )


def pick(values, index, axis):
    return lax.dynamic_index_in_dim(values, index, axis, keepdims=False)


def paired(bit, own, peer, axis):
    return ordered(bit, jnp.expand_dims(own, axis), jnp.expand_dims(peer, axis), axis)


def by_z(place, pieces, axis):
    step = 1
    groups = [jnp.expand_dims(piece, axis) for piece in pieces]
    while step < place.depth:
        bit = (place.z // step) % 2
        groups = [
            ordered(bit, groups[2 * i], groups[2 * i + 1], axis) for i in range(len(groups) // 2)
        ]
        step *= 2
    return groups[0]


def spread_z(place, piece, axis):
    pieces = [piece] + [swap_z(piece, step) for step in range(1, place.depth)]
    return by_z(place, pieces, axis)


def gather_start(place, stack, half):
    first, second = stack[..., :half], stack[..., half:]
    return paired(place.y, first, swap_y(first), 1), paired(place.x, second, swap_x(second), 0)


def gather_finish(place, first, second):
    first = paired(place.x, first, swap_x(first), 0)
    second = paired(place.y, second, swap_y(second), 2)
    return first.reshape(-1, first.shape[-1]), second.reshape(-1, second.shape[-1])


def after(values, *others):
    return lax.optimization_barrier((values,) + others)[0]


def add(first, second):
    return (first.astype(F32) + second.astype(F32)).astype(BF16)


def halve(blocks, bit, dim, send):
    return pick(blocks, bit, dim), send(pick(blocks, 1 - bit, dim))


def scatter_far(place, first, second):
    rows = first.shape[0] // place.chips
    first, second = (
        grads.reshape(2, place.depth, 2, rows, grads.shape[1]) for grads in (first, second)
    )
    return halve(first, place.x, 0, swap_x), halve(second, place.y, 2, swap_y)


def scatter_near(place, first, second):
    return halve(add(*first), place.y, 1, swap_y), halve(add(*second), place.x, 0, swap_x)


def scatter_z(place, first, second):
    part = jnp.concatenate([add(*first), add(*second)], axis=-1)
    return [pick(part, place.z, 0)] + [
        swap_z(pick(part, place.z ^ step, 0), step) for step in range(1, place.depth)
    ]


def total(pieces):
    return sum(piece.astype(F32) for piece in pieces)


def rope(values, cosine, sine):
    return values * cosine + pltpu.roll(values, HEAD_SIZE // 2, 1) * sine


def rope_back(grads, cosine, sine):
    return grads * cosine + pltpu.roll(grads * sine, HEAD_SIZE // 2, 1)


def row_scale(values):
    return lax.rsqrt(jnp.mean(values * values, axis=-1, keepdims=True) + EPSILON)


def head(ref, index):
    return ref[:, index * HEAD_SIZE : (index + 1) * HEAD_SIZE]


def dot_t(left, right):
    return lax.dot_general(left, right, (((1,), (1,)), ((), ())), preferred_element_type=F32)


def t_dot(left, right):
    return lax.dot_general(left, right, (((0,), (0,)), ((), ())), preferred_element_type=F32)


def allowed_keys(position):
    row = lax.broadcasted_iota(jnp.int32, (MB_TOK, MB_TOK), 0)
    key = lax.broadcasted_iota(jnp.int32, (MB_TOK, MB_TOK), 1)
    allowed = (key <= row) & (key >= row - position)
    return jnp.concatenate([allowed] * QUERIES_PER_KEY, axis=0)


def attend_kernel(q_ref, kv_ref, cos_ref, sin_ref, pos_ref, qg_ref, kg_ref, out_ref):
    heads = kv_ref.shape[1] // (2 * HEAD_SIZE)
    cosine, sine = cos_ref[...], sin_ref[...]
    allowed = allowed_keys(pos_ref[...])
    for j in range(heads):
        keys = head(kv_ref, j)
        key_low = rope(keys * row_scale(keys) * kg_ref[...], cosine, sine).astype(BF16)
        value = head(kv_ref, heads + j).astype(BF16)
        queries = []
        for g in range(QUERIES_PER_KEY):
            query = head(q_ref, QUERIES_PER_KEY * j + g)
            queries.append(
                rope(query * row_scale(query) * qg_ref[...], cosine, sine).astype(BF16)
            )
        scores = dot_t(jnp.concatenate(queries, axis=0), key_low) * SCALE
        scores = jnp.where(allowed, scores, MASKED)
        expo = jnp.exp(scores - jnp.max(scores, axis=-1, keepdims=True))
        probs = (expo / jnp.sum(expo, axis=-1, keepdims=True)).astype(BF16)
        mixed = jnp.dot(probs, value, preferred_element_type=F32).astype(BF16)
        for g in range(QUERIES_PER_KEY):
            index = QUERIES_PER_KEY * j + g
            out_ref[:, index * HEAD_SIZE : (index + 1) * HEAD_SIZE] = mixed[
                g * MB_TOK : (g + 1) * MB_TOK
            ]


def attend_back_kernel(
    q_ref, kv_ref, cos_ref, sin_ref, pos_ref, qg_ref, kg_ref, datt_ref,
    dq_ref, dkv_ref, sum_q_ref, sum_k_ref,
):
    heads = kv_ref.shape[1] // (2 * HEAD_SIZE)
    cosine, sine = cos_ref[...], sin_ref[...]
    allowed = allowed_keys(pos_ref[...])

    @pl.when(pl.program_id(0) == 0)
    def _():
        sum_q_ref[...] = jnp.zeros_like(sum_q_ref)
        sum_k_ref[...] = jnp.zeros_like(sum_k_ref)

    def normed_back(grad_low, raw, scale, gain):
        grad = rope_back(grad_low, cosine, sine)
        term = jnp.sum((grad * raw * scale).reshape(-1, 8, HEAD_SIZE), axis=0)
        weighted = grad * gain
        back = scale * weighted - raw * (scale * scale * scale) * jnp.mean(
            weighted * raw, axis=-1, keepdims=True
        )
        return back, term

    for j in range(heads):
        keys = head(kv_ref, j)
        key_scale = row_scale(keys)
        key_low = rope(keys * key_scale * kg_ref[...], cosine, sine).astype(BF16)
        value = head(kv_ref, heads + j).astype(BF16)
        raws, scales, lows, datts = [], [], [], []
        for g in range(QUERIES_PER_KEY):
            query = head(q_ref, QUERIES_PER_KEY * j + g)
            scale = row_scale(query)
            raws.append(query)
            scales.append(scale)
            lows.append(rope(query * scale * qg_ref[...], cosine, sine).astype(BF16))
            datts.append(head(datt_ref, QUERIES_PER_KEY * j + g))
        low = jnp.concatenate(lows, axis=0)
        datt = jnp.concatenate(datts, axis=0)
        scores = jnp.where(allowed, dot_t(low, key_low) * SCALE, MASKED)
        expo = jnp.exp(scores - jnp.max(scores, axis=-1, keepdims=True))
        probs = expo / jnp.sum(expo, axis=-1, keepdims=True)
        dprobs = dot_t(datt, value)
        dscores = (
            probs * (dprobs - jnp.sum(probs * dprobs, axis=-1, keepdims=True))
        ).astype(BF16)
        dlow = jnp.dot(dscores, key_low, preferred_element_type=F32) * SCALE
        dkey = t_dot(dscores, low) * SCALE
        dvalue = t_dot(probs.astype(BF16), datt)
        for g in range(QUERIES_PER_KEY):
            index = QUERIES_PER_KEY * j + g
            back, term = normed_back(
                dlow[g * MB_TOK : (g + 1) * MB_TOK], raws[g], scales[g], qg_ref[...]
            )
            dq_ref[:, index * HEAD_SIZE : (index + 1) * HEAD_SIZE] = back.astype(BF16)
            sum_q_ref[...] += term
        back, term = normed_back(dkey, keys, key_scale, kg_ref[...])
        dkv_ref[:, j * HEAD_SIZE : (j + 1) * HEAD_SIZE] = back.astype(BF16)
        sum_k_ref[...] += term
        index = heads + j
        dkv_ref[:, index * HEAD_SIZE : (index + 1) * HEAD_SIZE] = dvalue.astype(BF16)


def rows_spec(width):
    return pl.BlockSpec((MB_TOK, width), lambda i: (i, 0))


def same_spec(rows, width):
    return pl.BlockSpec((rows, width), lambda i: (0, 0))


def attend(q, kv, cosine, sine, position, q_gain, k_gain):
    tokens, q_width = q.shape
    kv_width = kv.shape[1]
    return pl.pallas_call(
        attend_kernel,
        grid=(tokens // MB_TOK,),
        in_specs=[rows_spec(q_width), rows_spec(kv_width)]
        + [rows_spec(HEAD_SIZE)] * 3
        + [same_spec(1, HEAD_SIZE)] * 2,
        out_specs=rows_spec(q_width),
        out_shape=jax.ShapeDtypeStruct((tokens, q_width), BF16),
        name="attend",
    )(q, kv, cosine, sine, position, q_gain, k_gain)


def attend_back(q, kv, cosine, sine, position, q_gain, k_gain, datt):
    tokens, q_width = q.shape
    kv_width = kv.shape[1]
    return pl.pallas_call(
        attend_back_kernel,
        grid=(tokens // MB_TOK,),
        in_specs=[rows_spec(q_width), rows_spec(kv_width)]
        + [rows_spec(HEAD_SIZE)] * 3
        + [same_spec(1, HEAD_SIZE)] * 2
        + [rows_spec(q_width)],
        out_specs=[
            rows_spec(q_width),
            rows_spec(kv_width),
            same_spec(8, HEAD_SIZE),
            same_spec(8, HEAD_SIZE),
        ],
        out_shape=[
            jax.ShapeDtypeStruct((tokens, q_width), BF16),
            jax.ShapeDtypeStruct((tokens, kv_width), BF16),
            jax.ShapeDtypeStruct((8, HEAD_SIZE), F32),
            jax.ShapeDtypeStruct((8, HEAD_SIZE), F32),
        ],
        name="attend_back",
    )(q, kv, cosine, sine, position, q_gain, k_gain, datt)


def rope_tables(position):
    half_width = HEAD_SIZE // 2
    frequency = ROPE_BASE ** (-2.0 * jnp.arange(half_width, dtype=F32) / HEAD_SIZE)
    angles = position[:, None] * frequency[None, :]
    cosine, sine = jnp.cos(angles), jnp.sin(angles)
    return (
        jnp.concatenate([cosine, cosine], axis=-1),
        jnp.concatenate([-sine, sine], axis=-1),
    )


def on_device(
    tokens_in,
    grad_out,
    seq_lengths,
    seq_deal,
    norm_attn,
    query_key_value_weight,
    query_norm_gain,
    k_gain,
    output_weight,
    norm_mlp,
    w_gate_up,
    w_down,
):
    place = Place()
    core = place.core
    tok_dev, width = tokens_in.shape
    query_width = QUERY_HEADS * HEAD_SIZE
    kv_width = KEY_VALUE_HEADS * HEAD_SIZE
    q_half, kv_half, out_half = query_width // 2, kv_width // 2, width // 2
    ff_block = w_down.shape[0]
    ff_half = ff_block * place.chips

    rows = query_key_value_weight.shape[0]

    def qkv_half(side):
        return jnp.concatenate(
            [
                lax.dynamic_slice_in_dim(query_key_value_weight, side * q_half, q_half, 1),
                lax.dynamic_slice_in_dim(
                    query_key_value_weight, query_width + side * kv_half, kv_half, 1
                ),
                lax.dynamic_slice_in_dim(
                    query_key_value_weight, query_width + kv_width + side * kv_half, kv_half, 1
                ),
            ],
            axis=1,
        )

    gain_rows, head_rows = norm_attn.shape[0], query_norm_gain.shape[0]
    small = jnp.concatenate([norm_attn, norm_mlp, query_norm_gain, k_gain])
    small_count = small.shape[0]
    lanes = small_count + -small_count % 128
    small = jnp.pad(small[None, :], ((0, rows - 1), (0, lanes - small_count)))

    def with_small(side):
        return jnp.concatenate([qkv_half(side), small], axis=1)

    qkv_piece = ordered(core, with_small(core), swap_core(with_small(1 - core)), 0)
    out_piece = ordered(
        core,
        lax.dynamic_slice_in_dim(output_weight, core * out_half, out_half, 1),
        swap_core(lax.dynamic_slice_in_dim(output_weight, (1 - core) * out_half, out_half, 1)),
        0,
    )
    qkv_first = (w_gate_up, grad_out, tokens_in, seq_lengths, seq_deal)
    w_gate_up, grad_out, tokens_in, seq_lengths, seq_deal = after(qkv_first, qkv_piece)
    gate_split = w_gate_up.reshape(rows, 2, place.chips, 2, ff_block)
    gate_split = gate_split.transpose(3, 0, 1, 2, 4).reshape(2, rows, 2 * ff_half)
    gate_piece = ordered(core, pick(gate_split, core, 0), swap_core(pick(gate_split, 1 - core, 0)), 0)

    def own(values):
        return lax.dynamic_slice_in_dim(values, core * tok_dev, tok_dev, 0)

    def peer(values):
        return lax.dynamic_slice_in_dim(values, (1 - core) * tok_dev, tok_dev, 0)

    first_row = place.x * tok_dev
    own_rows = first_row + jnp.arange(tok_dev, dtype=jnp.int32)
    source, own_position = deal_rows(seq_lengths[0], seq_deal[0], own_rows)
    peer_tokens = swap_x(tokens_in)
    x_own = take_rows(tokens_in, peer_tokens, source, first_row).astype(BF16)
    x_low = ordered(core, x_own, swap_core(x_own), 0)
    own_position = own_position.astype(F32)
    position = ordered(core, own_position, swap_core(own_position), 0)
    grads_low = ordered(core, grad_out, swap_core(grad_out), 0)

    qkv_stack = spread_z(place, qkv_piece, 0)
    gate_piece = after(gate_piece, qkv_stack)
    gate_pieces = [gate_piece] + [swap_z(gate_piece, step) for step in range(1, place.depth)]
    qkv_parts = gather_start(place, qkv_stack, q_half)
    gate_stack = by_z(place, after(gate_pieces, *qkv_parts), 0)
    w_q, w_kv = gather_finish(place, *qkv_parts)
    w_gate, w_up = gather_finish(place, *gather_start(place, gate_stack, ff_half))
    w_out = lax.all_gather(out_piece, CHIPS, axis=0, tiled=True)
    w_low = lax.all_gather(w_down, CHIPS, axis=0, tiled=True)

    gains = w_kv[:, 2 * kv_half :].reshape(2 * place.chips, rows, lanes)[:, 0].astype(F32)
    w_kv = w_kv[:, : 2 * kv_half]
    gain_one = gains[:, :gain_rows].reshape(1, width)
    gain_two = gains[:, gain_rows : 2 * gain_rows].reshape(1, width)
    gain_q = gains[:, 2 * gain_rows : 2 * gain_rows + head_rows].reshape(1, HEAD_SIZE)
    gain_k = gains[:, 2 * gain_rows + head_rows : small_count].reshape(1, HEAD_SIZE)

    cosine, sine = rope_tables(position)
    position_wide = jnp.broadcast_to(position.astype(jnp.int32)[:, None], (2 * tok_dev, MB_TOK))

    x = x_low.astype(F32)
    scale_one = row_scale(x)
    normed_one = (x * scale_one * gain_one).astype(BF16)
    q = jnp.dot(normed_one, w_q, preferred_element_type=F32)
    kv = jnp.dot(normed_one, w_kv, preferred_element_type=F32)
    att = attend(q, kv, cosine, sine, position_wide, gain_q, gain_k)
    att_peer = swap_core(att)
    w_out_own = lax.dynamic_slice_in_dim(w_out, core * q_half, q_half, 0)
    w_out_peer = lax.dynamic_slice_in_dim(w_out, (1 - core) * q_half, q_half, 0)
    delta = (
        jnp.dot(att, w_out_own, preferred_element_type=F32)
        + jnp.dot(att_peer, w_out_peer, preferred_element_type=F32)
    ).astype(BF16)
    residual = x + ordered(core, delta, swap_core(delta), 1).astype(F32)
    scale_two = row_scale(residual)
    normed_two = (residual * scale_two * gain_two).astype(BF16)
    gate = jnp.dot(normed_two, w_gate, preferred_element_type=F32)
    up = jnp.dot(normed_two, w_up, preferred_element_type=F32)
    sigmoid = jax.nn.sigmoid(gate)
    activated = (gate * sigmoid * up).astype(BF16)
    down = jnp.dot(activated, w_low, preferred_element_type=F32)
    y_out = (
        own(residual) + own(down) + swap_core(peer(down).astype(BF16)).astype(F32)
    ).astype(BF16)

    term_down = t_dot(activated, grads_low).astype(BF16)
    out_down = lax.psum_scatter(term_down, CHIPS, scatter_dimension=0, tiled=True).astype(F32)
    grad_act = dot_t(grads_low, w_low)
    grad_gate = (grad_act * up * (sigmoid * (1.0 + gate * (1.0 - sigmoid)))).astype(BF16)
    grad_up = (grad_act * (gate * sigmoid)).astype(BF16)
    term_gate = t_dot(normed_two, grad_gate).astype(BF16)
    term_up = t_dot(normed_two, grad_up).astype(BF16)
    gate_far = scatter_far(place, term_gate, term_up)
    part_two = dot_t(grad_gate, w_gate) + dot_t(grad_up, w_up)
    grad_normed_two = part_two + swap_core(part_two.astype(BF16)).astype(F32)
    term_norm_two = jnp.sum(own(grad_normed_two * residual * scale_two), axis=0)
    grad_residual = grads_low.astype(F32) + norm_back(
        grad_normed_two, residual, scale_two, gain_two
    )
    branch = grad_residual.astype(BF16)
    branch_own = lax.dynamic_slice_in_dim(branch, core * out_half, out_half, 1)
    datt = (
        dot_t(branch_own, w_out_own)
        + swap_core(dot_t(branch_own, w_out_peer).astype(BF16)).astype(F32)
    ).astype(BF16)
    term_out_own = t_dot(att, branch_own).astype(BF16)
    term_out_peer = t_dot(att_peer, branch_own).astype(BF16)
    term_out = ordered(core, term_out_own, term_out_peer, 0)
    out_quarter = out_half // 2
    out_far = scatter_far(place, term_out[:, :out_quarter], term_out[:, out_quarter:])
    dq, dkv, sum_q, sum_k = attend_back(
        q, kv, cosine, sine, position_wide, gain_q, gain_k, datt
    )
    gate_near = scatter_near(place, *after(gate_far, dq))
    out_near = scatter_near(place, *after(out_far, gate_near[0][0], gate_near[1][0]))
    term_q = t_dot(normed_one, dq).astype(BF16)
    term_kv = t_dot(normed_one, dkv).astype(BF16)
    part_one = dot_t(dq, w_q) + dot_t(dkv, w_kv)
    grad_normed_one = own(part_one) + swap_core(peer(part_one).astype(BF16)).astype(F32)
    x_first, scale_first = own(x), own(scale_one)
    term_norm_one = jnp.sum(grad_normed_one * x_first * scale_first, axis=0)
    grad_dealt = (
        own(grad_residual) + norm_back(grad_normed_one, x_first, scale_first, gain_one)
    ).astype(BF16)
    devices = 2 * place.chips
    sums = jnp.concatenate(
        [
            term_norm_one.reshape(devices, gain_rows),
            term_norm_two.reshape(devices, gain_rows),
            jnp.sum(sum_q, axis=0).reshape(devices, head_rows),
            jnp.sum(sum_k, axis=0).reshape(devices, head_rows),
        ],
        axis=1,
    )
    sums = jnp.pad(sums[:, None, :], ((0, 0), (0, rows - 1), (0, lanes - small_count)))
    sums = sums.reshape(devices * rows, lanes).astype(BF16)
    qkv_far = scatter_far(place, term_q, jnp.concatenate([term_kv, sums], axis=1))
    gate_last = scatter_z(place, *after(gate_near, qkv_far[0][0]))
    out_last = scatter_z(place, *after(out_near, gate_last[0]))
    qkv_near = scatter_near(place, *qkv_far)
    out_gate = total(after(gate_last, qkv_near[0][0], qkv_near[1][0]))
    qkv_last = scatter_z(place, *qkv_near)
    out_out = total(out_last)
    target = back_rows(seq_lengths[0], seq_deal[0], own_rows)
    grad_in = take_rows(grad_dealt, swap_x(grad_dealt), target, first_row)

    def unsplit(chip_rows, device_rows):
        chip_rows = chip_rows.reshape(2, device_rows, chip_rows.shape[1])
        return paired(core, pick(chip_rows, core, 0), swap_core(pick(chip_rows, 1 - core, 0)), 1)

    grad_out_proj = unsplit(out_out, output_weight.shape[0]).reshape(output_weight.shape)
    both = unsplit(out_gate, rows)
    grad_gate_up = (
        both.reshape(rows, 2, 2, place.chips, ff_block)
        .transpose(0, 2, 3, 1, 4)
        .reshape(rows, w_gate_up.shape[1])
    )
    qkv_last = after(qkv_last, grad_gate_up, grad_out_proj, grad_in)
    both = unsplit(total(qkv_last), rows)
    grad_qkv = jnp.concatenate(
        [
            both[:, :, :q_half].reshape(rows, query_width),
            both[:, :, q_half : q_half + kv_half].reshape(rows, kv_width),
            both[:, :, q_half + kv_half : q_half + 2 * kv_half].reshape(rows, kv_width),
        ],
        axis=1,
    )
    owned = jnp.sum(both[0, :, q_half + 2 * kv_half :], axis=0)
    return (
        y_out,
        grad_in,
        owned[:gain_rows],
        grad_qkv,
        owned[2 * gain_rows : 2 * gain_rows + head_rows],
        owned[2 * gain_rows + head_rows : small_count],
        grad_out_proj,
        owned[gain_rows : 2 * gain_rows],
        grad_gate_up,
        out_down,
    )


def norm_back(grad_norm, inputs, scale, gain):
    weighted = grad_norm * gain
    return scale * weighted - inputs * (scale * scale * scale) * jnp.mean(
        weighted * inputs, axis=-1, keepdims=True
    )


def solution(mesh):
    groups, size = mesh.shape["grp"], mesh.shape["dp"]
    mesh = jax.sharding.Mesh(mesh.devices.reshape(groups, size // 4, 2, 2), DEVICES)
    rows, line, pairs = P(DEVICES, None), P(DEVICES), P(("z", "y", "core"), None)
    return jax.shard_map(
        on_device,
        mesh=mesh,
        in_specs=(rows, rows, pairs, pairs, line, rows, line, line, rows, line, rows, rows),
        out_specs=(rows, rows, line, rows, line, line, rows, line, rows, rows),
        check_vma=False,
    )
```
